1024 devices in a mesh: gx: 32 (over y_lo, z), gy: 32 (over x, y_hi, core).
Axes of the slice: x: 4, y: 8 (y_hi: 4, y_lo: 2; y = y_hi * 2 + y_lo), z: 16, core: 2. Of those that a mesh axis runs over, the one named last changes fastest.
Arguments:
- hamiltonian: float32 [32, 32, 5, 128, 128], P('gx', 'gy'), may hold values from -0.25 to 0.25
- inverse_margin: float32 [32, 32, 5, 128, 128], P('gx', 'gy'), may hold values from -0.25 to 0.25
- density: float32 [2, 32, 32, 5, 128, 128], P(None, 'gx', 'gy'), may hold values from -6 to 6
- cutoff: int32 [32, 32, 5], P('gx', 'gy'), may hold values 0 or 1
- derivative: float32 [3, 32, 32, 5, 128, 128], P(None, 'gx', 'gy'), may hold values from -0.046875 to 0.046875
- atom_of: int32 [32, 32, 128], P('gx', 'gy'), may hold values from 0 to 63, as said below
Outputs:
- new_density: float32 [2, 32, 32, 5, 128, 128], P(None, 'gx', 'gy')
- forces: float32 [32, 32, 3, 64], P('gx', 'gy')
The draws below stay inside these ranges and needn't reach their ends.
Inputs may be any that keep to these rules, and one draw needn't show every extreme that they name: `atom_of`: within each group the map never falls and each of the 64 atoms owns at least one of the 128 orbitals.
All inputs are finite; a program needn't handle non-finite values. No bound on the sum of `cutoff` on one device may be relied on, other than what follows from the above.
Results may differ from the reference program's by a relative error of at most 0.0001.
Values sent between devices are 32-bit elements; how exact they have to be, the bound alone decides.
A program may use at most 64 MiB of HBM per device.

```python
import jax
import jax.numpy as jnp
from jax import lax

B = 128
ATOMS = 64
STEPS = 1
CELLS_X = 32
CELLS_Y = 32


def draw_atom_of(key, part):
    scores = jax.random.randint(key, (CELLS_X, CELLS_Y, B - 1), 0, 1048576)
    scores = scores * B + jnp.arange(B - 1, dtype=jnp.int32)
    ranks = jnp.argsort(jnp.argsort(scores, axis=-1), axis=-1)
    breaks = (ranks < ATOMS - 1).astype(jnp.int32)
    counted = jnp.cumsum(breaks, axis=-1).astype(jnp.int32)
    first = jnp.zeros((CELLS_X, CELLS_Y, 1), jnp.int32)
    return jnp.concatenate([first, counted], axis=-1)


def set_ends(array, own_key, low, high):
    shape = array.shape
    place = [jax.random.randint(jax.random.fold_in(own_key, axis), (), 0, shape[axis]) for axis in range(len(shape))]
    array = array.at[tuple(place)].set(low)
    longest = shape.index(max(shape))
    place[longest] = (place[longest] + 1) % shape[longest]
    return array.at[tuple(place)].set(high)


def block_scale(rng, dims, shards, low, largest):
    gain, own = 1.0, jax.random.fold_in(rng, 6)
    for axis_at, blocks in shards:
        draws = jnp.exp(jax.random.uniform(jax.random.fold_in(own, axis_at), (blocks,), jnp.float32, low / len(shards), largest / len(shards)))
        gain = gain * jnp.repeat(draws, dims[axis_at] // blocks).reshape([-1 if axis == axis_at else 1 for axis in range(len(dims))])
    return gain


def gaussian(stream_key, shape, scale, bound, cuts=(), kind=jnp.bfloat16):
    values = jax.random.normal(stream_key, shape, jnp.float32) * scale
    if len(cuts) > 0:
        values = block_scale(stream_key, shape, cuts, -0.22, 0.18) * values
    return jnp.clip(values, min=-bound, max=bound).astype(kind)


def setup_inputs(seed: int = 0) -> dict:
    streams_of = jax.random.split(jax.random.key(seed), 7)
    return {
        "hamiltonian": gaussian(streams_of[0], (CELLS_X, CELLS_Y, 5, B, B), (5 * B) ** -0.5, 0.25, ((0, 32), (1, 32)), jnp.float32),
        "inverse_margin": gaussian(streams_of[1], (CELLS_X, CELLS_Y, 5, B, B), (5 * B) ** -0.5, 0.25, ((0, 32), (1, 32)), jnp.float32),
        "density": gaussian(streams_of[2], (2, CELLS_X, CELLS_Y, 5, B, B), 1.0, 6.0, ((1, 32), (2, 32)), jnp.float32),
        "cutoff": set_ends((jax.random.randint(streams_of[3], (CELLS_X, CELLS_Y, 5), 0, 4) < 3).astype(jnp.int32), jax.random.fold_in(streams_of[3], 1), 0, 1),
        "derivative": gaussian(streams_of[4], (3, CELLS_X, CELLS_Y, 5, B, B), (1.0 / B), 0.046875, ((1, 32), (2, 32)), jnp.float32),
        "atom_of": draw_atom_of(jax.random.fold_in(streams_of[6], 71), 0),
    }


opposite = (0, 2, 1, 4, 3)
time_step = 0.25
highest = lax.Precision.HIGHEST


def neighbour_row(block, offset):
    if offset == 1:
        return jnp.roll(block, -1, 0)
    if offset == 2:
        return jnp.roll(block, 1, 0)
    if offset == 3:
        return jnp.roll(block, -1, 1)
    return jnp.roll(block, 1, 1)


def block_mul(left, right):
    return jnp.einsum("xyuv,xyvw->xyuw", left, right, precision=highest)


def product(left, right, keep):
    diagonal = block_mul(left[:, :, 0], right[:, :, 0])
    others = []
    for offset in range(1, 5):
        diagonal = diagonal + block_mul(left[:, :, offset], neighbour_row(right[:, :, opposite[offset]], offset))
        others.append(block_mul(left[:, :, 0], right[:, :, offset]) + block_mul(left[:, :, offset], neighbour_row(right[:, :, 0], offset)))
    return jnp.stack([diagonal] + others, axis=2) * keep[:, :, :, None, None]


def reference(hamiltonian, inverse_margin, density, cutoff, derivative, atom_of):
    keep = jnp.concatenate([jnp.ones_like(cutoff[:, :, :1]), cutoff[:, :, 1:]], axis=2).astype(jnp.float32)
    weight = keep[:, :, :, None, None]
    ham = hamiltonian * weight
    inverse = inverse_margin * weight
    real_part = density[0] * weight
    imag_part = density[1] * weight
    propagator = product(inverse, ham, keep)
    for step in range(STEPS):
        real_comm = product(propagator, real_part, keep) - product(product(real_part, ham, keep), inverse, keep)
        imag_comm = product(propagator, imag_part, keep) - product(product(imag_part, ham, keep), inverse, keep)
        real_part, imag_part = real_part + time_step * imag_comm, imag_part - time_step * real_comm
    members = (atom_of[:, :, None, :] == jnp.arange(ATOMS, dtype=jnp.int32)[None, None, :, None]).astype(jnp.float32)
    results = []
    for direction in range(3):
        weighted = real_part * (derivative[direction] * weight)
        row_part = jnp.sum(weighted, axis=(2, 4))
        column_part = jnp.sum(weighted, axis=3)
        orbital = row_part + column_part[:, :, 0]
        orbital = orbital + jnp.roll(column_part[:, :, 1], 1, 0) + jnp.roll(column_part[:, :, 2], -1, 0)
        orbital = orbital + jnp.roll(column_part[:, :, 3], 1, 1) + jnp.roll(column_part[:, :, 4], -1, 1)
        results.append(-jnp.einsum("xyaw,xyw->xya", members, orbital, precision=highest))
    forces = jnp.stack(results, axis=2)
    return jnp.stack([real_part, imag_part], 0), forces
```

```python
import jax
import jax.numpy as jnp
from jax import lax
from jax.experimental import pallas as pl
from jax.experimental.pallas import tpu as pltpu
from jax.sharding import PartitionSpec as P

B = 128
ATOMS = 64
time_step = 0.25
MESH = pl.DeviceIdType.MESH
f32, bf16 = jnp.float32, jnp.bfloat16

H, S, R, I = 0, 1, 2, 3
opposite = (0, 2, 1, 4, 3)


def split(x):
    high = x.astype(bf16)
    return high, (x - high.astype(f32)).astype(bf16)


def dot(a, b):
    return jnp.dot(a, b, preferred_element_type=f32)


def multiply(ah, al, bh, bl):
    return dot(ah, bh) + (dot(ah, bl) + dot(al, bh))


def neighbour(offset):
    axis = "gx" if offset <= 2 else "gy"
    count = lax.axis_size(axis)
    step = 1 if offset in (1, 3) else count - 1
    return {axis: lax.rem(lax.axis_index(axis) + step, count)}


def kernel(
    ham, inv, den, cut_hbm, der, atom_hbm,
    out, forces,
    cut, atom, own, slope, send, recv, col_send, col_recv,
    left_h, left_l, hb_h, hb_l, pair_h, pair_l, first, mixed_h, mixed_l, comm,
    in_sem, small_sem, der_sem, send_sem, recv_sem, cs_sem, cr_sem,
):
    barrier = pltpu.get_barrier_semaphore()
    places = {o: neighbour(o) for o in (1, 2, 3, 4)}
    for o in (1, 2, 3, 4):
        pl.semaphore_signal(barrier, inc=1, device_id=places[o], device_id_type=MESH)

    load_cut = pltpu.make_async_copy(cut_hbm, cut, small_sem.at[0])
    load_cut.start()
    load_atom = pltpu.make_async_copy(atom_hbm, atom, small_sem.at[1])
    load_atom.start()
    sources = {H: ham.at[0, 0], S: inv.at[0, 0], R: den.at[0, 0, 0], I: den.at[1, 0, 0]}
    loads = {}
    for m in (H, S, I, R):
        loads[m] = pltpu.make_async_copy(sources[m], own.at[m], in_sem.at[m])
        loads[m].start()
    load_slope = pltpu.make_async_copy(der.at[:, 0, 0], slope, der_sem)
    load_slope.start()

    load_cut.wait()
    keep = [None] + [cut[0, 0, o].astype(f32) for o in (1, 2, 3, 4)]

    def prepare(m):
        loads[m].wait()
        for o in range(5):
            block = own[m, o]
            if o > 0:
                block = block * keep[o]
                send[m, o - 1, 1] = block
                own[m, o] = block
            else:
                for p in range(4):
                    send[m, p, 0] = block
            high, low = split(block)
            columns = pl.ds(o * B, B)
            if m == H:
                hb_h[:, columns] = high
                hb_l[:, columns] = low
            else:
                rows = pl.ds((m - 1) * B, B)
                left_h[o, rows, :] = high
                left_l[o, rows, :] = low
                if m == S:
                    for t in range(2):
                        pair_h[t, pl.ds(B, B), columns] = high
                        pair_l[t, pl.ds(B, B), columns] = low
                else:
                    pair_h[m - 2, pl.ds(0, B), columns] = high
                    pair_l[m - 2, pl.ds(0, B), columns] = low

    copies = {}

    def transfer(m, o):
        copies[m, o] = pltpu.make_async_remote_copy(
            src_ref=send.at[m, o - 1],
            dst_ref=recv.at[m, opposite[o] - 1],
            send_sem=send_sem.at[m, o - 1],
            recv_sem=recv_sem.at[m, opposite[o] - 1],
            device_id=places[o],
            device_id_type=MESH,
        )
        copies[m, o].start()

    def arrived(m, o):
        copies[m, opposite[o]].wait_recv()

    order = (1, 2, 3, 4)
    prepare(H)
    pl.semaphore_wait(barrier, 4)
    for o in order:
        transfer(H, o)
    prepare(S)
    for o in order:
        transfer(S, o)
    prepare(I)
    for o in order:
        transfer(I, o)
    prepare(R)
    for o in order:
        transfer(R, o)

    for o in range(5):
        columns = pl.ds(o * B, B)
        first[o] = multiply(left_h[0], left_l[0], hb_h[:, columns], hb_l[:, columns])

    for o in order:
        arrived(H, o)
        near = jnp.concatenate([recv[H, o - 1, 0], recv[H, o - 1, 1]], axis=1)
        bh, bl = split(near)
        part = multiply(left_h[o], left_l[o], bh, bl)
        first[0] += part[:, B:]
        row = (first[o] + part[:, :B]) * keep[o]
        for t, sign in ((0, 1.0), (1, -1.0), (2, -1.0)):
            high, low = split(row[t * B : (t + 1) * B] * sign)
            mixed_h[o, :, pl.ds(t * B, B)] = high
            mixed_l[o, :, pl.ds(t * B, B)] = low
    for t, sign in ((0, 1.0), (1, -1.0), (2, -1.0)):
        high, low = split(first[0, pl.ds(t * B, B), :] * sign)
        mixed_h[0, :, pl.ds(t * B, B)] = high
        mixed_l[0, :, pl.ds(t * B, B)] = low

    def lefts(o, m):
        t = m - 1
        return (
            jnp.concatenate([mixed_h[o, :, pl.ds(0, B)], mixed_h[o, :, pl.ds(t * B, B)]], axis=1),
            jnp.concatenate([mixed_l[o, :, pl.ds(0, B)], mixed_l[o, :, pl.ds(t * B, B)]], axis=1),
        )

    def commutator(m):
        ah, al = lefts(0, m)
        for o in range(5):
            columns = pl.ds(o * B, B)
            comm[o] = multiply(ah, al, pair_h[m - 2, :, columns], pair_l[m - 2, :, columns])
        for o in order:
            if m == I:
                arrived(S, o)
            arrived(m, o)
            near = jnp.concatenate(
                [
                    jnp.concatenate([recv[m, o - 1, 0], recv[m, o - 1, 1]], axis=1),
                    jnp.concatenate([recv[S, o - 1, 0], recv[S, o - 1, 1]], axis=1),
                ],
                axis=0,
            )
            bh, bl = split(near)
            ah, al = lefts(o, m)
            part = multiply(ah, al, bh, bl)
            comm[0] += part[:, B:]
            comm[o] = (comm[o] + part[:, :B]) * keep[o]

    commutator(I)
    for o in range(5):
        out[0, 0, 0, o] = own[R, o] + time_step * comm[o]

    load_slope.wait()
    sends = []
    for o in order:
        block = out[0, 0, 0, o]
        for c in range(3):
            col_send[o - 1, pl.ds(c, 1), :] = jnp.sum(block * slope[c, o], axis=0, keepdims=True)
        sends.append(
            pltpu.make_async_remote_copy(
                src_ref=col_send.at[o - 1],
                dst_ref=col_recv.at[o - 1],
                send_sem=cs_sem.at[o - 1],
                recv_sem=cr_sem.at[o - 1],
                device_id=places[o],
                device_id_type=MESH,
            )
        )
        sends[-1].start()

    commutator(R)
    for o in range(5):
        out[1, 0, 0, o] = own[I, o] - time_step * comm[o]

    rows, cols = [], []
    for c in range(3):
        weighted = out[0, 0, 0, 0] * slope[c, 0]
        cols.append(jnp.sum(weighted, axis=0, keepdims=True))
        for o in order:
            weighted = weighted + out[0, 0, 0, o] * slope[c, o]
        rows.append(jnp.sum(weighted.T, axis=0, keepdims=True))
    orbital = jnp.concatenate(rows, axis=0) + jnp.concatenate(cols, axis=0)
    load_atom.wait()
    members = (
        jnp.broadcast_to(atom[0], (ATOMS, B)) == lax.broadcasted_iota(jnp.int32, (ATOMS, B), 0)
    ).astype(f32)
    for copy in sends:
        copy.wait_recv()
    for o in order:
        orbital = orbital + col_recv[o - 1, pl.ds(0, 3), :]
    total = -lax.dot_general(
        orbital, members, (((1,), (1,)), ((), ())),
        precision=lax.Precision.HIGHEST, preferred_element_type=f32,
    )
    for c in range(3):
        forces[0, c] = total[c : c + 1]
    for copy in copies.values():
        copy.wait_send()
    for copy in sends:
        copy.wait_send()


def local(hamiltonian, inverse_margin, density, cutoff, derivative, atom_of):
    hbm = pl.BlockSpec(memory_space=pltpu.HBM)
    vmem = pl.BlockSpec(memory_space=pltpu.VMEM)
    dma = pltpu.SemaphoreType.DMA
    density, forces = pl.pallas_call(
        kernel,
        out_shape=(
            jax.ShapeDtypeStruct((2, 1, 1, 5, B, B), f32),
            jax.ShapeDtypeStruct((1, 3, 1, ATOMS), f32),
        ),
        in_specs=[hbm] * 6,
        out_specs=(vmem, vmem),
        scratch_shapes=[
            pltpu.SMEM((1, 1, 5), jnp.int32),
            pltpu.VMEM((1, 1, B), jnp.int32),
            pltpu.VMEM((4, 5, B, B), f32),
            pltpu.VMEM((3, 5, B, B), f32),
            pltpu.VMEM((4, 4, 2, B, B), f32),
            pltpu.VMEM((4, 4, 2, B, B), f32),
            pltpu.VMEM((4, 8, B), f32),
            pltpu.VMEM((4, 8, B), f32),
            pltpu.VMEM((5, 3 * B, B), bf16),
            pltpu.VMEM((5, 3 * B, B), bf16),
            pltpu.VMEM((B, 5 * B), bf16),
            pltpu.VMEM((B, 5 * B), bf16),
            pltpu.VMEM((2, 2 * B, 5 * B), bf16),
            pltpu.VMEM((2, 2 * B, 5 * B), bf16),
            pltpu.VMEM((5, 3 * B, B), f32),
            pltpu.VMEM((5, B, 3 * B), bf16),
            pltpu.VMEM((5, B, 3 * B), bf16),
            pltpu.VMEM((5, B, B), f32),
            dma((4,)),
            dma((2,)),
            dma,
            dma((4, 4)),
            dma((4, 4)),
            dma((4,)),
            dma((4,)),
        ],
        compiler_params=pltpu.CompilerParams(
            collective_id=0, has_side_effects=True, vmem_limit_bytes=40 * 1024 * 1024
        ),
        name="cell",
    )(*[
        pltpu.with_memory_space_constraint(x, pltpu.HBM)
        for x in (hamiltonian, inverse_margin, density, cutoff, derivative, atom_of)
    ])
    return density, forces.reshape(1, 1, 3, ATOMS)


def solution(mesh):
    placed = (
        P("gx", "gy", None, None, None),
        P("gx", "gy", None, None, None),
        P(None, "gx", "gy", None, None, None),
        P("gx", "gy", None),
        P(None, "gx", "gy", None, None, None),
        P("gx", "gy", None),
    )
    return jax.shard_map(
        local,
        mesh=mesh,
        in_specs=placed,
        out_specs=(P(None, "gx", "gy", None, None, None), P("gx", "gy", None, None)),
        check_vma=False,
    )
```

```python
import jax
import jax.numpy as jnp
from jax import lax
from jax.experimental import pallas as pl
from jax.experimental.pallas import tpu as pltpu
from jax.sharding import PartitionSpec as P

B = 128
ATOMS = 64
time_step = 0.25
MESH = pl.DeviceIdType.MESH
f32, bf16 = jnp.float32, jnp.bfloat16

H, S, R, I = 0, 1, 2, 3
STAGED = (H, S)
opposite = (0, 2, 1, 4, 3)


def split(x):
    high = x.astype(bf16)
    return high, (x - high.astype(f32)).astype(bf16)


def dot(a, b):
    return jnp.dot(a, b, preferred_element_type=f32)


def multiply(ah, al, bh, bl):
    return dot(ah, bh) + (dot(ah, bl) + dot(al, bh))


def neighbour(offset):
    axis = "gx" if offset <= 2 else "gy"
    count = lax.axis_size(axis)
    step = 1 if offset in (1, 3) else count - 1
    return {axis: lax.rem(lax.axis_index(axis) + step, count)}


def kernel(
    ham, inv, den, cut_hbm, der, atom_hbm,
    out, forces,
    cut, atom, own, slope, send, recv, col_send, col_recv,
    left_h, left_l, hb_h, hb_l, pair_h, pair_l, hams, mixed_h, mixed_l, comm,
    in_sem, small_sem, der_sem, send_sem, recv_sem, cs_sem, cr_sem, passing, pass_sem, forward_sem,
):
    barrier = pltpu.get_barrier_semaphore()
    places = {o: neighbour(o) for o in (1, 2, 3, 4)}

    count = lax.axis_size("gx")
    half = count // 2
    row, line = lax.axis_index("gx"), lax.axis_index("gy")

    def is_early(place):
        at_row, at_line = place.get("gx", row), place.get("gy", line)
        return (lax.rem(at_row, half) == 0) & ((at_row > 0) | (at_line > 0))

    early = is_early({})
    late = jnp.logical_not(early)
    near_early = {o: is_early(places[o]) for o in (1, 2, 3, 4)}
    near_late = {o: jnp.logical_not(near_early[o]) for o in (1, 2, 3, 4)}
    paired = (lax.rem(row, half) == 0) & (line > 0)
    served = (lax.rem(row, half) == half - 1) & (line > 0)
    twin = {"gx": lax.rem(row + half, count)}
    behind = {"gx": lax.rem(row + half - 1, count)}
    ahead = {"gx": lax.rem(row + half + 1, count)}

    def greet(place, condition):
        @pl.when(condition)
        def _():
            pl.semaphore_signal(barrier, inc=1, device_id=place, device_id_type=MESH)

    for o in (1, 2, 3, 4):
        greet(places[o], early == near_early[o])
    greet(twin, paired)

    load_cut = pltpu.make_async_copy(cut_hbm, cut, small_sem.at[0])
    load_cut.start()
    load_atom = pltpu.make_async_copy(atom_hbm, atom, small_sem.at[1])
    load_atom.start()
    sources = {H: ham.at[0, 0], S: inv.at[0, 0], R: den.at[0, 0, 0], I: den.at[1, 0, 0]}
    loads = {}
    for m in (H, S, I, R):
        loads[m] = pltpu.make_async_copy(sources[m], own.at[m], in_sem.at[m])
        loads[m].start()
    load_slope = pltpu.make_async_copy(der.at[:, 0, 0], slope, der_sem)
    load_slope.start()

    load_cut.wait()
    keep = [None] + [cut[0, 0, o].astype(f32) for o in (1, 2, 3, 4)]

    def prepare(m):
        loads[m].wait()
        for o in range(5):
            block = own[m, o]
            if o > 0:
                block = block * keep[o]
                send[m, o - 1, 1] = block
                own[m, o] = block
            else:
                for p in range(4):
                    send[m, p, 0] = block
            high, low = split(block)
            columns = pl.ds(o * B, B)
            if m == H:
                hb_h[:, columns] = high
                hb_l[:, columns] = low
            else:
                rows = pl.ds((m - 1) * B, B)
                left_h[o, rows, :] = high
                left_l[o, rows, :] = low
                if m == S:
                    for t in range(2):
                        pair_h[t, pl.ds(B, B), columns] = high
                        pair_l[t, pl.ds(B, B), columns] = low
                else:
                    pair_h[m - 2, pl.ds(0, B), columns] = high
                    pair_l[m - 2, pl.ds(0, B), columns] = low

    def copy(m, o):
        return pltpu.make_async_remote_copy(
            src_ref=send.at[m, o - 1],
            dst_ref=recv.at[m, opposite[o] - 1],
            send_sem=send_sem.at[m, o - 1],
            recv_sem=recv_sem.at[m, opposite[o] - 1],
            device_id=places[o],
            device_id_type=MESH,
        )

    def arrived(m, o):
        copy(m, opposite[o]).wait_recv()

    order = (3, 4, 1, 2)

    as_one = paired.astype(jnp.int32)
    heard = near_early[3].astype(jnp.int32) + near_early[4].astype(jnp.int32) + as_one

    @pl.when(early)
    def _():
        pl.semaphore_wait(barrier, heard)

    for o in (1, 2, 3, 4):
        greet(places[o], early & near_late[o])
    greet(behind, paired)

    prepare(H)

    @pl.when(late)
    def _():
        pl.semaphore_wait(barrier, 4 + served.astype(jnp.int32))

    for o in (1, 2, 3, 4):
        greet(places[o], late & near_early[o])
    greet(ahead, served)

    def to_twin(m):
        return pltpu.make_async_remote_copy(
            src_ref=send.at[m, 1],
            dst_ref=passing.at[m],
            send_sem=send_sem.at[m, 1],
            recv_sem=pass_sem.at[m],
            device_id=twin,
            device_id_type=MESH,
        )

    def forward(m):
        return pltpu.make_async_remote_copy(
            src_ref=passing.at[m],
            dst_ref=recv.at[m, 0],
            send_sem=forward_sem.at[m],
            recv_sem=recv_sem.at[m, 0],
            device_id=behind,
            device_id_type=MESH,
        )

    def transfer(m, o, condition):
        if o == 2 and m in STAGED:
            condition = condition & jnp.logical_not(paired)

        @pl.when(condition)
        def _():
            copy(m, o).start()

    def launch(m):
        for o in (1, 2, 3, 4):
            transfer(m, o, late | near_early[o])
        if m in STAGED:

            @pl.when(paired)
            def _():
                to_twin(m).start()

    launch(H)
    for m in (S, I, R):
        prepare(m)
        launch(m)

    @pl.when(early)
    def _():
        pl.semaphore_wait(barrier, 4 + 2 * as_one - heard)
        for m in (H, S, I, R):
            for o in (1, 2, 3, 4):
                transfer(m, o, near_late[o])
            if m in STAGED:

                @pl.when(paired)
                def _():
                    to_twin(m).wait_recv()
                    forward(m).start()

    for o in range(5):
        columns = pl.ds(o * B, B)
        hams[o] = multiply(left_h[0], left_l[0], hb_h[:, columns], hb_l[:, columns])

    for o in order:
        arrived(H, o)
        near = jnp.concatenate([recv[H, o - 1, 0], recv[H, o - 1, 1]], axis=1)
        bh, bl = split(near)
        part = multiply(left_h[o], left_l[o], bh, bl)
        hams[0] += part[:, B:]
        block = (hams[o] + part[:, :B]) * keep[o]
        for t, sign in ((0, 1.0), (1, -1.0), (2, -1.0)):
            high, low = split(block[t * B : (t + 1) * B] * sign)
            mixed_h[o, :, pl.ds(t * B, B)] = high
            mixed_l[o, :, pl.ds(t * B, B)] = low
    for t, sign in ((0, 1.0), (1, -1.0), (2, -1.0)):
        high, low = split(hams[0, pl.ds(t * B, B), :] * sign)
        mixed_h[0, :, pl.ds(t * B, B)] = high
        mixed_l[0, :, pl.ds(t * B, B)] = low

    def lefts(o, m):
        t = m - 1
        return (
            jnp.concatenate([mixed_h[o, :, pl.ds(0, B)], mixed_h[o, :, pl.ds(t * B, B)]], axis=1),
            jnp.concatenate([mixed_l[o, :, pl.ds(0, B)], mixed_l[o, :, pl.ds(t * B, B)]], axis=1),
        )

    def commutator(m):
        ah, al = lefts(0, m)
        for o in range(5):
            columns = pl.ds(o * B, B)
            comm[o] = multiply(ah, al, pair_h[m - 2, :, columns], pair_l[m - 2, :, columns])
        for o in order:
            if m == I:
                arrived(S, o)
            arrived(m, o)
            near = jnp.concatenate(
                [
                    jnp.concatenate([recv[m, o - 1, 0], recv[m, o - 1, 1]], axis=1),
                    jnp.concatenate([recv[S, o - 1, 0], recv[S, o - 1, 1]], axis=1),
                ],
                axis=0,
            )
            bh, bl = split(near)
            ah, al = lefts(o, m)
            part = multiply(ah, al, bh, bl)
            comm[0] += part[:, B:]
            comm[o] = (comm[o] + part[:, :B]) * keep[o]

    commutator(I)
    for o in range(5):
        out[0, 0, 0, o] = own[R, o] + time_step * comm[o]

    load_slope.wait()
    sends = []
    for o in order:
        block = out[0, 0, 0, o]
        for c in range(3):
            col_send[o - 1, pl.ds(c, 1), :] = jnp.sum(block * slope[c, o], axis=0, keepdims=True)
        sends.append(
            pltpu.make_async_remote_copy(
                src_ref=col_send.at[o - 1],
                dst_ref=col_recv.at[o - 1],
                send_sem=cs_sem.at[o - 1],
                recv_sem=cr_sem.at[o - 1],
                device_id=places[o],
                device_id_type=MESH,
            )
        )
        sends[-1].start()

    commutator(R)
    for o in range(5):
        out[1, 0, 0, o] = own[I, o] - time_step * comm[o]

    rows, cols = [], []
    for c in range(3):
        weighted = out[0, 0, 0, 0] * slope[c, 0]
        cols.append(jnp.sum(weighted, axis=0, keepdims=True))
        for o in order:
            weighted = weighted + out[0, 0, 0, o] * slope[c, o]
        rows.append(jnp.sum(weighted.T, axis=0, keepdims=True))
    orbital = jnp.concatenate(rows, axis=0) + jnp.concatenate(cols, axis=0)
    load_atom.wait()
    members = (
        jnp.broadcast_to(atom[0], (ATOMS, B)) == lax.broadcasted_iota(jnp.int32, (ATOMS, B), 0)
    ).astype(f32)
    for item in sends:
        item.wait_recv()
    for o in order:
        orbital = orbital + col_recv[o - 1, pl.ds(0, 3), :]
    total = -lax.dot_general(
        orbital, members, (((1,), (1,)), ((), ())),
        precision=lax.Precision.HIGHEST, preferred_element_type=f32,
    )
    for c in range(3):
        forces[0, c] = total[c : c + 1]
    for m in (H, S, I, R):
        for o in order:
            copy(m, o).wait_send()
    for item in sends:
        item.wait_send()

    @pl.when(paired)
    def _():
        for m in STAGED:
            forward(m).wait_send()


def local(hamiltonian, inverse_margin, density, cutoff, derivative, atom_of):
    hbm = pl.BlockSpec(memory_space=pltpu.HBM)
    vmem = pl.BlockSpec(memory_space=pltpu.VMEM)
    dma = pltpu.SemaphoreType.DMA
    density, forces = pl.pallas_call(
        kernel,
        out_shape=(
            jax.ShapeDtypeStruct((2, 1, 1, 5, B, B), f32),
            jax.ShapeDtypeStruct((1, 3, 1, ATOMS), f32),
        ),
        in_specs=[hbm] * 6,
        out_specs=(vmem, vmem),
        scratch_shapes=[
            pltpu.SMEM((1, 1, 5), jnp.int32),
            pltpu.VMEM((1, 1, B), jnp.int32),
            pltpu.VMEM((4, 5, B, B), f32),
            pltpu.VMEM((3, 5, B, B), f32),
            pltpu.VMEM((4, 4, 2, B, B), f32),
            pltpu.VMEM((4, 4, 2, B, B), f32),
            pltpu.VMEM((4, 8, B), f32),
            pltpu.VMEM((4, 8, B), f32),
            pltpu.VMEM((5, 3 * B, B), bf16),
            pltpu.VMEM((5, 3 * B, B), bf16),
            pltpu.VMEM((B, 5 * B), bf16),
            pltpu.VMEM((B, 5 * B), bf16),
            pltpu.VMEM((2, 2 * B, 5 * B), bf16),
            pltpu.VMEM((2, 2 * B, 5 * B), bf16),
            pltpu.VMEM((5, 3 * B, B), f32),
            pltpu.VMEM((5, B, 3 * B), bf16),
            pltpu.VMEM((5, B, 3 * B), bf16),
            pltpu.VMEM((5, B, B), f32),
            dma((4,)),
            dma((2,)),
            dma,
            dma((4, 4)),
            dma((4, 4)),
            dma((4,)),
            dma((4,)),
            pltpu.VMEM((4, 2, B, B), f32),
            dma((4,)),
            dma((4,)),
        ],
        compiler_params=pltpu.CompilerParams(
            collective_id=0, has_side_effects=True, vmem_limit_bytes=40 * 1024 * 1024
        ),
        name="cell",
    )(*[
        pltpu.with_memory_space_constraint(x, pltpu.HBM)
        for x in (hamiltonian, inverse_margin, density, cutoff, derivative, atom_of)
    ])
    return density, forces.reshape(1, 1, 3, ATOMS)


def solution(mesh):
    placed = (
        P("gx", "gy", None, None, None),
        P("gx", "gy", None, None, None),
        P(None, "gx", "gy", None, None, None),
        P("gx", "gy", None),
        P(None, "gx", "gy", None, None, None),
        P("gx", "gy", None),
    )
    return jax.shard_map(
        local,
        mesh=mesh,
        in_specs=placed,
        out_specs=(P(None, "gx", "gy", None, None, None), P("gx", "gy", None, None)),
        check_vma=False,
    )
```

```python
import jax
import jax.numpy as jnp
from jax import lax
from jax.experimental import pallas as pl
from jax.experimental.pallas import tpu as pltpu
from jax.sharding import PartitionSpec as P

B = 128
ATOMS = 64
time_step = 0.25
MESH = pl.DeviceIdType.MESH
f32, bf16 = jnp.float32, jnp.bfloat16

H, S, R, I = 0, 1, 2, 3
BY_TWIN = (H, S)
opposite = (0, 2, 1, 4, 3)


def split(x):
    high = x.astype(bf16)
    return high, (x - high.astype(f32)).astype(bf16)


def dot(a, b):
    return jnp.dot(a, b, preferred_element_type=f32)


def multiply(ah, al, bh, bl):
    return dot(ah, bh) + (dot(ah, bl) + dot(al, bh))


def neighbour(offset):
    axis = "gx" if offset <= 2 else "gy"
    count = lax.axis_size(axis)
    step = 1 if offset in (1, 3) else count - 1
    return {axis: lax.rem(lax.axis_index(axis) + step, count)}


def kernel(
    ham, inv, den, cut_hbm, der, atom_hbm,
    out, forces,
    cut, atom, own, slope, send, recv, col_send, col_recv,
    left_h, left_l, hb_h, hb_l, pair_h, pair_l, hams, mixed_h, mixed_l, comm,
    in_sem, small_sem, der_sem, send_sem, recv_sem, cs_sem, cr_sem, passing, pass_sem, forward_sem,
):
    barrier = pltpu.get_barrier_semaphore()
    places = {o: neighbour(o) for o in (1, 2, 3, 4)}

    count = lax.axis_size("gx")
    half = count // 2
    row, line = lax.axis_index("gx"), lax.axis_index("gy")

    def is_front(place):
        return lax.rem(place.get("gx", row), half) == 0

    def is_lead(place):
        return (place.get("gx", row) == 0) & (place.get("gy", line) == 0)

    def along(step):
        return {"gx": lax.rem(row + step, count)}

    front, lead = is_front({}), is_lead({})
    early, late = front & jnp.logical_not(lead), jnp.logical_not(front)
    near_front = {o: is_front(places[o]) for o in (1, 2, 3, 4)}
    near_lead = {o: is_lead(places[o]) for o in (1, 2, 3, 4)}
    beside = early & (near_lead[3] | near_lead[4])
    depth = lax.rem(row, half)
    paired = front & (line > 0)
    carrier = (depth == 1) & (line > 0)
    served = (depth == half - 1) & (line > 0)
    twin, cousin, behind = along(half), along(half + 1), along(half - 1)
    giver, taker = along(half - 1), along(half - 2)
    ahead, helper = along(half + 1), along(half + 2)

    def number(condition):
        return condition.astype(jnp.int32)

    def greet(place, condition):
        @pl.when(condition)
        def _():
            pl.semaphore_signal(barrier, inc=1, device_id=place, device_id_type=MESH)

    def await_greetings(condition, amount):
        @pl.when(condition)
        def _():
            pl.semaphore_wait(barrier, amount)

    for o in (1, 2):
        greet(places[o], late & jnp.logical_not(near_front[o]))
    for o in (3, 4):
        greet(places[o], late | (early & jnp.logical_not(near_lead[o])))
    greet(twin, paired)

    load_cut = pltpu.make_async_copy(cut_hbm, cut, small_sem.at[0])
    load_cut.start()
    load_atom = pltpu.make_async_copy(atom_hbm, atom, small_sem.at[1])
    load_atom.start()
    sources = {H: ham.at[0, 0], S: inv.at[0, 0], R: den.at[0, 0, 0], I: den.at[1, 0, 0]}
    loads = {}
    for m in (H, S, I, R):
        loads[m] = pltpu.make_async_copy(sources[m], own.at[m], in_sem.at[m])
        loads[m].start()
    load_slope = pltpu.make_async_copy(der.at[:, 0, 0], slope, der_sem)
    load_slope.start()

    load_cut.wait()
    keep = [None] + [cut[0, 0, o].astype(f32) for o in (1, 2, 3, 4)]

    def prepare(m):
        loads[m].wait()
        for o in range(5):
            block = own[m, o]
            if o > 0:
                block = block * keep[o]
                send[m, o - 1, 1] = block
                own[m, o] = block
            else:
                for p in range(4):
                    send[m, p, 0] = block
            high, low = split(block)
            columns = pl.ds(o * B, B)
            if m == H:
                hb_h[:, columns] = high
                hb_l[:, columns] = low
            else:
                rows = pl.ds((m - 1) * B, B)
                left_h[o, rows, :] = high
                left_l[o, rows, :] = low
                if m == S:
                    for t in range(2):
                        pair_h[t, pl.ds(B, B), columns] = high
                        pair_l[t, pl.ds(B, B), columns] = low
                else:
                    pair_h[m - 2, pl.ds(0, B), columns] = high
                    pair_l[m - 2, pl.ds(0, B), columns] = low

    def copy(m, o):
        return pltpu.make_async_remote_copy(
            src_ref=send.at[m, o - 1],
            dst_ref=recv.at[m, opposite[o] - 1],
            send_sem=send_sem.at[m, o - 1],
            recv_sem=recv_sem.at[m, opposite[o] - 1],
            device_id=places[o],
            device_id_type=MESH,
        )

    def arrived(m, o):
        copy(m, opposite[o]).wait_recv()

    order = (3, 4, 1, 2)

    await_greetings(early, 2 - number(beside) + number(paired))
    await_greetings(lead, 2)
    for o in (3, 4):
        greet(places[o], lead)
    greet(places[1], front)
    greet(cousin, paired)
    prepare(H)
    await_greetings(late, 4 + number(carrier) + 2 * number(served))
    for o in (1, 2):
        greet(places[o], late & near_front[o])
    greet(giver, carrier)
    greet(taker, carrier)
    greet(ahead, served)
    greet(helper, served)

    def hand_on(m):
        return pltpu.make_async_remote_copy(
            src_ref=send.at[m, 1],
            dst_ref=passing.at[m],
            send_sem=send_sem.at[m, 1],
            recv_sem=pass_sem.at[m],
            device_id=twin if m in BY_TWIN else cousin,
            device_id_type=MESH,
        )

    def forward(m):
        return pltpu.make_async_remote_copy(
            src_ref=passing.at[m],
            dst_ref=recv.at[m, 0],
            send_sem=forward_sem.at[m],
            recv_sem=recv_sem.at[m, 0],
            device_id=behind if m in BY_TWIN else taker,
            device_id_type=MESH,
        )

    def transfer(m, o, condition):
        @pl.when(condition)
        def _():
            copy(m, o).start()

    def pass_on(m):
        hand_on(m).wait_recv()
        forward(m).start()

    def launch(m, which):
        for o in (1, 2):
            transfer(m, o, late & which)
        for o in (3, 4):
            transfer(m, o, jnp.logical_not(early & near_lead[o]) & which)
        if m in BY_TWIN:

            @pl.when(paired)
            def _():
                hand_on(m).start()

    launch(H, True)
    for m in (S, I):
        prepare(m)
        launch(m, True)
    prepare(R)
    launch(R, front)

    await_greetings(front, 1 + number(paired))
    for m in (H, S, I, R):
        transfer(m, 1, front)
        if m not in BY_TWIN:

            @pl.when(paired)
            def _():
                hand_on(m).start()

    for o in (3, 4):
        greet(places[o], early & near_lead[o])
    await_greetings(beside, 1)
    for o in (3, 4):
        for m in (H, S, I, R):
            transfer(m, o, early & near_lead[o])

    greet(places[2], front)
    greet(behind, paired)
    await_greetings(front, 1 + number(paired))
    for m in (H, S, I):
        transfer(m, 2, front & jnp.logical_not(paired))
    for m in BY_TWIN:

        @pl.when(paired)
        def _():
            pass_on(m)

    for o in range(5):
        columns = pl.ds(o * B, B)
        hams[o] = multiply(left_h[0], left_l[0], hb_h[:, columns], hb_l[:, columns])

    for o in order:
        arrived(H, o)
        near = jnp.concatenate([recv[H, o - 1, 0], recv[H, o - 1, 1]], axis=1)
        bh, bl = split(near)
        part = multiply(left_h[o], left_l[o], bh, bl)
        hams[0] += part[:, B:]
        block = (hams[o] + part[:, :B]) * keep[o]
        for t, sign in ((0, 1.0), (1, -1.0), (2, -1.0)):
            high, low = split(block[t * B : (t + 1) * B] * sign)
            mixed_h[o, :, pl.ds(t * B, B)] = high
            mixed_l[o, :, pl.ds(t * B, B)] = low
    for t, sign in ((0, 1.0), (1, -1.0), (2, -1.0)):
        high, low = split(hams[0, pl.ds(t * B, B), :] * sign)
        mixed_h[0, :, pl.ds(t * B, B)] = high
        mixed_l[0, :, pl.ds(t * B, B)] = low

    def lefts(o, m):
        t = m - 1
        return (
            jnp.concatenate([mixed_h[o, :, pl.ds(0, B)], mixed_h[o, :, pl.ds(t * B, B)]], axis=1),
            jnp.concatenate([mixed_l[o, :, pl.ds(0, B)], mixed_l[o, :, pl.ds(t * B, B)]], axis=1),
        )

    def commutator(m):
        ah, al = lefts(0, m)
        for o in range(5):
            columns = pl.ds(o * B, B)
            comm[o] = multiply(ah, al, pair_h[m - 2, :, columns], pair_l[m - 2, :, columns])
        if m == I:
            @pl.when(late)
            def _():
                for o in (1, 2, 3, 4):
                    copy(I, o).wait_send()
                    copy(R, o).start()

        for o in order:
            if m == I:
                arrived(S, o)
            arrived(m, o)
            near = jnp.concatenate(
                [
                    jnp.concatenate([recv[m, o - 1, 0], recv[m, o - 1, 1]], axis=1),
                    jnp.concatenate([recv[S, o - 1, 0], recv[S, o - 1, 1]], axis=1),
                ],
                axis=0,
            )
            bh, bl = split(near)
            ah, al = lefts(o, m)
            part = multiply(ah, al, bh, bl)
            comm[0] += part[:, B:]
            comm[o] = (comm[o] + part[:, :B]) * keep[o]

    commutator(I)
    transfer(R, 2, front & jnp.logical_not(paired))
    for o in range(5):
        out[0, 0, 0, o] = own[R, o] + time_step * comm[o]

    load_slope.wait()
    sends = []
    for o in order:
        block = out[0, 0, 0, o]
        for c in range(3):
            col_send[o - 1, pl.ds(c, 1), :] = jnp.sum(block * slope[c, o], axis=0, keepdims=True)
        sends.append(
            pltpu.make_async_remote_copy(
                src_ref=col_send.at[o - 1],
                dst_ref=col_recv.at[o - 1],
                send_sem=cs_sem.at[o - 1],
                recv_sem=cr_sem.at[o - 1],
                device_id=places[o],
                device_id_type=MESH,
            )
        )
        sends[-1].start()

    @pl.when(carrier)
    def _():
        pl.semaphore_wait(barrier, 1)
        for m in (I, R, S, H):
            if m not in BY_TWIN:
                pass_on(m)

    commutator(R)
    for o in range(5):
        out[1, 0, 0, o] = own[I, o] - time_step * comm[o]

    rows, cols = [], []
    for c in range(3):
        weighted = out[0, 0, 0, 0] * slope[c, 0]
        cols.append(jnp.sum(weighted, axis=0, keepdims=True))
        for o in order:
            weighted = weighted + out[0, 0, 0, o] * slope[c, o]
        rows.append(jnp.sum(weighted.T, axis=0, keepdims=True))
    orbital = jnp.concatenate(rows, axis=0) + jnp.concatenate(cols, axis=0)
    load_atom.wait()
    members = (
        jnp.broadcast_to(atom[0], (ATOMS, B)) == lax.broadcasted_iota(jnp.int32, (ATOMS, B), 0)
    ).astype(f32)
    for item in sends:
        item.wait_recv()
    for o in order:
        orbital = orbital + col_recv[o - 1, pl.ds(0, 3), :]
    total = -lax.dot_general(
        orbital, members, (((1,), (1,)), ((), ())),
        precision=lax.Precision.HIGHEST, preferred_element_type=f32,
    )
    for c in range(3):
        forces[0, c] = total[c : c + 1]
    for m in (H, S, R):
        for o in order:
            copy(m, o).wait_send()

    @pl.when(front)
    def _():
        for o in order:
            copy(I, o).wait_send()

    for item in sends:
        item.wait_send()

    for m in (H, S, I, R):

        @pl.when(paired if m in BY_TWIN else carrier)
        def _():
            forward(m).wait_send()


def local(hamiltonian, inverse_margin, density, cutoff, derivative, atom_of):
    hbm = pl.BlockSpec(memory_space=pltpu.HBM)
    vmem = pl.BlockSpec(memory_space=pltpu.VMEM)
    dma = pltpu.SemaphoreType.DMA
    density, forces = pl.pallas_call(
        kernel,
        out_shape=(
            jax.ShapeDtypeStruct((2, 1, 1, 5, B, B), f32),
            jax.ShapeDtypeStruct((1, 3, 1, ATOMS), f32),
        ),
        in_specs=[hbm] * 6,
        out_specs=(vmem, vmem),
        scratch_shapes=[
            pltpu.SMEM((1, 1, 5), jnp.int32),
            pltpu.VMEM((1, 1, B), jnp.int32),
            pltpu.VMEM((4, 5, B, B), f32),
            pltpu.VMEM((3, 5, B, B), f32),
            pltpu.VMEM((4, 4, 2, B, B), f32),
            pltpu.VMEM((4, 4, 2, B, B), f32),
            pltpu.VMEM((4, 8, B), f32),
            pltpu.VMEM((4, 8, B), f32),
            pltpu.VMEM((5, 3 * B, B), bf16),
            pltpu.VMEM((5, 3 * B, B), bf16),
            pltpu.VMEM((B, 5 * B), bf16),
            pltpu.VMEM((B, 5 * B), bf16),
            pltpu.VMEM((2, 2 * B, 5 * B), bf16),
            pltpu.VMEM((2, 2 * B, 5 * B), bf16),
            pltpu.VMEM((5, 3 * B, B), f32),
            pltpu.VMEM((5, B, 3 * B), bf16),
            pltpu.VMEM((5, B, 3 * B), bf16),
            pltpu.VMEM((5, B, B), f32),
            dma((4,)),
            dma((2,)),
            dma,
            dma((4, 4)),
            dma((4, 4)),
            dma((4,)),
            dma((4,)),
            pltpu.VMEM((4, 2, B, B), f32),
            dma((4,)),
            dma((4,)),
        ],
        compiler_params=pltpu.CompilerParams(
            collective_id=0, has_side_effects=True, vmem_limit_bytes=40 * 1024 * 1024
        ),
        name="cell",
    )(*[
        pltpu.with_memory_space_constraint(x, pltpu.HBM)
        for x in (hamiltonian, inverse_margin, density, cutoff, derivative, atom_of)
    ])
    return density, forces.reshape(1, 1, 3, ATOMS)


def solution(mesh):
    placed = (
        P("gx", "gy", None, None, None),
        P("gx", "gy", None, None, None),
        P(None, "gx", "gy", None, None, None),
        P("gx", "gy", None),
        P(None, "gx", "gy", None, None, None),
        P("gx", "gy", None),
    )
    return jax.shard_map(
        local,
        mesh=mesh,
        in_specs=placed,
        out_specs=(P(None, "gx", "gy", None, None, None), P("gx", "gy", None, None)),
        check_vma=False,
    )
```

```python
import jax
import jax.numpy as jnp
from jax import lax
from jax.experimental import pallas as pl
from jax.experimental.pallas import tpu as pltpu
from jax.sharding import PartitionSpec as P

B = 128
ATOMS = 64
time_step = 0.25
MESH = pl.DeviceIdType.MESH
f32, bf16 = jnp.float32, jnp.bfloat16

H, S, R, I = 0, 1, 2, 3
BY_TWIN = (H, S)
opposite = (0, 2, 1, 4, 3)


def split(x):
    high = x.astype(bf16)
    return high, (x - high.astype(f32)).astype(bf16)


def dot(a, b):
    return jnp.dot(a, b, preferred_element_type=f32)


def multiply(ah, al, bh, bl):
    return dot(ah, bh) + (dot(ah, bl) + dot(al, bh))


def neighbour(offset):
    axis = "gx" if offset <= 2 else "gy"
    count = lax.axis_size(axis)
    step = 1 if offset in (1, 3) else count - 1
    return {axis: lax.rem(lax.axis_index(axis) + step, count)}


def kernel(
    ham, inv, den, cut_hbm, der, atom_hbm,
    out, forces,
    cut, atom, own, slope, send, recv, col_send, col_recv,
    left_h, left_l, hb_h, hb_l, pair_h, pair_l, hams, mixed_h, mixed_l, comm,
    in_sem, small_sem, der_sem, send_sem, recv_sem, cs_sem, cr_sem, passing, pass_sem, forward_sem, side_h, side_l,
):
    barrier = pltpu.get_barrier_semaphore()
    places = {o: neighbour(o) for o in (1, 2, 3, 4)}

    count = lax.axis_size("gx")
    half = count // 2
    row, line = lax.axis_index("gx"), lax.axis_index("gy")

    def is_front(place):
        return lax.rem(place.get("gx", row), half) == 0

    def is_lead(place):
        return (place.get("gx", row) == 0) & (place.get("gy", line) == 0)

    def along(step):
        return {"gx": lax.rem(row + step, count)}

    front, lead = is_front({}), is_lead({})
    early, late = front & jnp.logical_not(lead), jnp.logical_not(front)
    near_front = {o: is_front(places[o]) for o in (1, 2, 3, 4)}
    near_lead = {o: is_lead(places[o]) for o in (1, 2, 3, 4)}
    beside = early & (near_lead[3] | near_lead[4])
    depth = lax.rem(row, half)
    paired = front & (line > 0)
    carrier = (depth == 1) & (line > 0)
    last = depth == half - 1
    served = last & (line > 0)
    twin, cousin, behind = along(half), along(half + 1), along(half - 1)
    giver, taker = along(half - 1), along(half - 2)
    ahead, helper = along(half + 1), along(half + 2)

    def number(condition):
        return condition.astype(jnp.int32)

    def greet(place, condition):
        @pl.when(condition)
        def _():
            pl.semaphore_signal(barrier, inc=1, device_id=place, device_id_type=MESH)

    def await_greetings(condition, amount):
        @pl.when(condition)
        def _():
            pl.semaphore_wait(barrier, amount)

    for o in (1, 2):
        greet(places[o], late & jnp.logical_not(near_front[o]))
    for o in (3, 4):
        greet(places[o], late | (early & jnp.logical_not(near_lead[o])))
    greet(twin, paired)

    load_cut = pltpu.make_async_copy(cut_hbm, cut, small_sem.at[0])
    load_cut.start()
    load_atom = pltpu.make_async_copy(atom_hbm, atom, small_sem.at[1])
    load_atom.start()
    sources = {H: ham.at[0, 0], S: inv.at[0, 0], R: den.at[0, 0, 0], I: den.at[1, 0, 0]}
    loads = {}
    for m in (H, S, I, R):
        loads[m] = pltpu.make_async_copy(sources[m], own.at[m], in_sem.at[m])
        loads[m].start()
    load_slope = pltpu.make_async_copy(der.at[:, 0, 0], slope, der_sem)
    load_slope.start()

    load_cut.wait()
    keep = [None] + [cut[0, 0, o].astype(f32) for o in (1, 2, 3, 4)]

    def prepare(m):
        loads[m].wait()
        for o in range(5):
            block = own[m, o]
            if o > 0:
                block = block * keep[o]
                send[m, o - 1, 1] = block
                own[m, o] = block
            else:
                for p in range(4):
                    send[m, p, 0] = block
            high, low = split(block)
            columns = pl.ds(o * B, B)
            if m == H:
                hb_h[:, columns] = high
                hb_l[:, columns] = low
            else:
                rows = pl.ds((m - 1) * B, B)
                left_h[o, rows, :] = high
                left_l[o, rows, :] = low
                if m == S:
                    for t in range(2):
                        pair_h[t, pl.ds(B, B), columns] = high
                        pair_l[t, pl.ds(B, B), columns] = low
                else:
                    pair_h[m - 2, pl.ds(0, B), columns] = high
                    pair_l[m - 2, pl.ds(0, B), columns] = low

    def copy(m, o):
        return pltpu.make_async_remote_copy(
            src_ref=send.at[m, o - 1],
            dst_ref=recv.at[m, opposite[o] - 1],
            send_sem=send_sem.at[m, o - 1],
            recv_sem=recv_sem.at[m, opposite[o] - 1],
            device_id=places[o],
            device_id_type=MESH,
        )

    def arrived(m, o):
        copy(m, opposite[o]).wait_recv()

    order = (3, 4, 1, 2)

    await_greetings(early, 2 - number(beside) + number(paired))
    await_greetings(lead, 2)
    for o in (3, 4):
        greet(places[o], lead)
    greet(places[1], front)
    greet(cousin, paired)
    prepare(H)
    await_greetings(late, 4 + number(carrier) + 2 * number(served))
    for o in (1, 2):
        greet(places[o], late & near_front[o])
    greet(giver, carrier)
    greet(taker, carrier)
    greet(ahead, served)
    greet(helper, served)

    def hand_on(m):
        return pltpu.make_async_remote_copy(
            src_ref=send.at[m, 1],
            dst_ref=passing.at[m],
            send_sem=send_sem.at[m, 1],
            recv_sem=pass_sem.at[m],
            device_id=twin if m in BY_TWIN else cousin,
            device_id_type=MESH,
        )

    def forward(m):
        return pltpu.make_async_remote_copy(
            src_ref=passing.at[m],
            dst_ref=recv.at[m, 0],
            send_sem=forward_sem.at[m],
            recv_sem=recv_sem.at[m, 0],
            device_id=behind if m in BY_TWIN else taker,
            device_id_type=MESH,
        )

    def transfer(m, o, condition):
        @pl.when(condition)
        def _():
            copy(m, o).start()

    def pass_on(m):
        hand_on(m).wait_recv()
        forward(m).start()

    def launch(m):
        for o in (1, 2):
            transfer(m, o, late)
        for o in (3, 4):
            transfer(m, o, jnp.logical_not(early & near_lead[o]) if m == H else front & jnp.logical_not(early & near_lead[o]))
        if m in BY_TWIN:

            @pl.when(paired)
            def _():
                hand_on(m).start()

    launch(H)
    for m in (S, I):
        prepare(m)
        launch(m)
    prepare(R)
    transfer(R, 1, last)
    for o in (3, 4):
        transfer(R, o, front & jnp.logical_not(early & near_lead[o]))

    await_greetings(front, 1 + number(paired))
    for m in (H, S, I, R):
        transfer(m, 1, front)
        if m not in BY_TWIN:

            @pl.when(paired)
            def _():
                hand_on(m).start()

    for o in (3, 4):
        greet(places[o], early & near_lead[o])
    await_greetings(beside, 1)
    for o in (3, 4):
        for m in (H, S, I, R):
            transfer(m, o, early & near_lead[o])

    greet(places[2], front)
    greet(behind, paired)
    await_greetings(front, 1 + number(paired))
    for m in (H, S, I):
        transfer(m, 2, front & jnp.logical_not(paired))
    for m in BY_TWIN:

        @pl.when(paired)
        def _():
            pass_on(m)

    for o in range(5):
        columns = pl.ds(o * B, B)
        hams[o] = multiply(left_h[0], left_l[0], hb_h[:, columns], hb_l[:, columns])

    @pl.when(late)
    def _():
        for o in (3, 4):
            copy(H, o).wait_send()
            copy(S, o).start()
            copy(I, o).start()

    for o in order:
        arrived(H, o)
        near = jnp.concatenate([recv[H, o - 1, 0], recv[H, o - 1, 1]], axis=1)
        bh, bl = split(near)
        part = multiply(left_h[o], left_l[o], bh, bl)
        hams[0] += part[:, B:]
        block = (hams[o] + part[:, :B]) * keep[o]
        for t, sign in ((0, 1.0), (1, -1.0), (2, -1.0)):
            high, low = split(block[t * B : (t + 1) * B] * sign)
            mixed_h[o, :, pl.ds(t * B, B)] = high
            mixed_l[o, :, pl.ds(t * B, B)] = low
    for t, sign in ((0, 1.0), (1, -1.0), (2, -1.0)):
        high, low = split(hams[0, pl.ds(t * B, B), :] * sign)
        mixed_h[0, :, pl.ds(t * B, B)] = high
        mixed_l[0, :, pl.ds(t * B, B)] = low

    def lefts(o, m):
        t = m - 1
        return (
            jnp.concatenate([mixed_h[o, :, pl.ds(0, B)], mixed_h[o, :, pl.ds(t * B, B)]], axis=1),
            jnp.concatenate([mixed_l[o, :, pl.ds(0, B)], mixed_l[o, :, pl.ds(t * B, B)]], axis=1),
        )

    def columns_to(o):
        return pltpu.make_async_remote_copy(
            src_ref=col_send.at[o - 1],
            dst_ref=col_recv.at[o - 1],
            send_sem=cs_sem.at[o - 1],
            recv_sem=cr_sem.at[o - 1],
            device_id=places[o],
            device_id_type=MESH,
        )

    def new_real(o):
        block = own[R, o] + time_step * comm[o]
        out[0, 0, 0, o] = block
        for c in range(3):
            col_send[o - 1, pl.ds(c, 1), :] = jnp.sum(block * slope[c, o], axis=0, keepdims=True)
        columns_to(o).start()
        transfer(R, o, late & jnp.logical_not(last) if o == 1 else late)

    def near(m, o):
        return split(jnp.concatenate([recv[m, o - 1, 0], recv[m, o - 1, 1]], axis=1))

    def mixed(o, t):
        return mixed_h[o, :, pl.ds(t * B, B)], mixed_l[o, :, pl.ds(t * B, B)]

    def commutator(m):
        ah, al = lefts(0, m)
        for o in range(5):
            columns = pl.ds(o * B, B)
            comm[o] = multiply(ah, al, pair_h[m - 2, :, columns], pair_l[m - 2, :, columns])
        for o in (1, 3, 4, 2):
            if m == I:
                arrived(S, o)
                sh, sl = near(S, o)
                side_h[o - 1], side_l[o - 1] = sh, sl
                arrived(I, o)
                bh, bl = near(I, o)
                part = multiply(*lefts(o, m), jnp.concatenate([bh, sh], axis=0), jnp.concatenate([bl, sl], axis=0))
                comm[0] += part[:, B:]
                comm[o] = (comm[o] + part[:, :B]) * keep[o]
                new_real(o)
            else:
                part = multiply(*mixed(o, 1), side_h[o - 1], side_l[o - 1])
                comm[0] += part[:, B:]
                comm[o] += part[:, :B]
        if m == R:
            for o in (1, 3, 4, 2):
                arrived(R, o)
                part = multiply(*mixed(o, 0), *near(R, o))
                comm[0] += part[:, B:]
                out[1, 0, 0, o] = own[I, o] - time_step * ((comm[o] + part[:, :B]) * keep[o])

    load_slope.wait()
    @pl.when(carrier)
    def _():
        pl.semaphore_wait(barrier, 1)
        for m in (I, R, S, H):
            if m not in BY_TWIN:
                pass_on(m)

    commutator(I)
    transfer(R, 2, front & jnp.logical_not(paired))
    out[0, 0, 0, 0] = own[R, 0] + time_step * comm[0]

    rows, cols = [], []
    for c in range(3):
        weighted = out[0, 0, 0, 0] * slope[c, 0]
        cols.append(jnp.sum(weighted, axis=0, keepdims=True))
        for o in order:
            weighted = weighted + out[0, 0, 0, o] * slope[c, o]
        rows.append(jnp.sum(weighted.T, axis=0, keepdims=True))
    orbital = jnp.concatenate(rows, axis=0) + jnp.concatenate(cols, axis=0)
    load_atom.wait()
    members = (
        jnp.broadcast_to(atom[0], (ATOMS, B)) == lax.broadcasted_iota(jnp.int32, (ATOMS, B), 0)
    ).astype(f32)
    commutator(R)
    out[1, 0, 0, 0] = own[I, 0] - time_step * comm[0]

    for o in order:
        columns_to(o).wait_recv()
    for o in order:
        orbital = orbital + col_recv[o - 1, pl.ds(0, 3), :]
    total = -lax.dot_general(
        orbital, members, (((1,), (1,)), ((), ())),
        precision=lax.Precision.HIGHEST, preferred_element_type=f32,
    )
    for c in range(3):
        forces[0, c] = total[c : c + 1]
    for m in (S, I, R):
        for o in order:
            copy(m, o).wait_send()
    for o in (1, 2):
        copy(H, o).wait_send()

    @pl.when(front)
    def _():
        for o in (3, 4):
            copy(H, o).wait_send()

    for o in order:
        columns_to(o).wait_send()

    for m in (H, S, I, R):

        @pl.when(paired if m in BY_TWIN else carrier)
        def _():
            forward(m).wait_send()


def local(hamiltonian, inverse_margin, density, cutoff, derivative, atom_of):
    hbm = pl.BlockSpec(memory_space=pltpu.HBM)
    vmem = pl.BlockSpec(memory_space=pltpu.VMEM)
    dma = pltpu.SemaphoreType.DMA
    density, forces = pl.pallas_call(
        kernel,
        out_shape=(
            jax.ShapeDtypeStruct((2, 1, 1, 5, B, B), f32),
            jax.ShapeDtypeStruct((1, 3, 1, ATOMS), f32),
        ),
        in_specs=[hbm] * 6,
        out_specs=(vmem, vmem),
        scratch_shapes=[
            pltpu.SMEM((1, 1, 5), jnp.int32),
            pltpu.VMEM((1, 1, B), jnp.int32),
            pltpu.VMEM((4, 5, B, B), f32),
            pltpu.VMEM((3, 5, B, B), f32),
            pltpu.VMEM((4, 4, 2, B, B), f32),
            pltpu.VMEM((4, 4, 2, B, B), f32),
            pltpu.VMEM((4, 8, B), f32),
            pltpu.VMEM((4, 8, B), f32),
            pltpu.VMEM((5, 3 * B, B), bf16),
            pltpu.VMEM((5, 3 * B, B), bf16),
            pltpu.VMEM((B, 5 * B), bf16),
            pltpu.VMEM((B, 5 * B), bf16),
            pltpu.VMEM((2, 2 * B, 5 * B), bf16),
            pltpu.VMEM((2, 2 * B, 5 * B), bf16),
            pltpu.VMEM((5, 3 * B, B), f32),
            pltpu.VMEM((5, B, 3 * B), bf16),
            pltpu.VMEM((5, B, 3 * B), bf16),
            pltpu.VMEM((5, B, B), f32),
            dma((4,)),
            dma((2,)),
            dma,
            dma((4, 4)),
            dma((4, 4)),
            dma((4,)),
            dma((4,)),
            pltpu.VMEM((4, 2, B, B), f32),
            dma((4,)),
            dma((4,)),
            pltpu.VMEM((4, B, 2 * B), bf16),
            pltpu.VMEM((4, B, 2 * B), bf16),
        ],
        compiler_params=pltpu.CompilerParams(
            collective_id=0, has_side_effects=True, vmem_limit_bytes=40 * 1024 * 1024
        ),
        name="cell",
    )(*[
        pltpu.with_memory_space_constraint(x, pltpu.HBM)
        for x in (hamiltonian, inverse_margin, density, cutoff, derivative, atom_of)
    ])
    return density, forces.reshape(1, 1, 3, ATOMS)


def solution(mesh):
    placed = (
        P("gx", "gy", None, None, None),
        P("gx", "gy", None, None, None),
        P(None, "gx", "gy", None, None, None),
        P("gx", "gy", None),
        P(None, "gx", "gy", None, None, None),
        P("gx", "gy", None),
    )
    return jax.shard_map(
        local,
        mesh=mesh,
        in_specs=placed,
        out_specs=(P(None, "gx", "gy", None, None, None), P("gx", "gy", None, None)),
        check_vma=False,
    )
```

```python
import jax
import jax.numpy as jnp
from jax import lax
from jax.experimental import pallas as pl
from jax.experimental.pallas import tpu as pltpu
from jax.sharding import PartitionSpec as P

B = 128
ATOMS = 64
time_step = 0.25
MESH = pl.DeviceIdType.MESH
f32, bf16 = jnp.float32, jnp.bfloat16

H, S, R, I = 0, 1, 2, 3
BY_TWIN = (H, S)
opposite = (0, 2, 1, 4, 3)


def split(x):
    high = x.astype(bf16)
    return high, (x - high.astype(f32)).astype(bf16)


def dot(a, b):
    return jnp.dot(a, b, preferred_element_type=f32)


def multiply(ah, al, bh, bl):
    return dot(ah, bh) + (dot(ah, bl) + dot(al, bh))


def neighbour(offset):
    axis = "gx" if offset <= 2 else "gy"
    count = lax.axis_size(axis)
    step = 1 if offset in (1, 3) else count - 1
    return {axis: lax.rem(lax.axis_index(axis) + step, count)}


def kernel(
    ham, inv, den, cut_hbm, der, atom_hbm,
    out, forces,
    cut, atom, own, slope, send, recv, col_send, col_recv,
    left_h, left_l, hb_h, hb_l, pair_h, pair_l, hams, mixed_h, mixed_l, comm,
    in_sem, small_sem, der_sem, send_sem, recv_sem, cs_sem, cr_sem, passing, pass_sem, forward_sem, side_h, side_l,
):
    barrier = pltpu.get_barrier_semaphore()
    places = {o: neighbour(o) for o in (1, 2, 3, 4)}

    count = lax.axis_size("gx")
    half = count // 2
    row, line = lax.axis_index("gx"), lax.axis_index("gy")

    def is_front(place):
        return lax.rem(place.get("gx", row), half) == 0

    def is_lead(place):
        return (place.get("gx", row) == 0) & (place.get("gy", line) == 0)

    def along(step):
        return {"gx": lax.rem(row + step, count)}

    front, lead = is_front({}), is_lead({})
    early, late = front & jnp.logical_not(lead), jnp.logical_not(front)
    near_front = {o: is_front(places[o]) for o in (1, 2, 3, 4)}
    near_lead = {o: is_lead(places[o]) for o in (1, 2, 3, 4)}
    beside = early & (near_lead[3] | near_lead[4])
    depth = lax.rem(row, half)
    paired = front & (line > 0)
    carrier = (depth == 1) & (line > 0)
    last = depth == half - 1
    served = last & (line > 0)
    twin, cousin, behind = along(half), along(half + 1), along(half - 1)
    giver, taker = along(half - 1), along(half - 2)
    ahead, helper = along(half + 1), along(half + 2)

    def number(condition):
        return condition.astype(jnp.int32)

    def greet(place, condition):
        @pl.when(condition)
        def _():
            pl.semaphore_signal(barrier, inc=1, device_id=place, device_id_type=MESH)

    def await_greetings(condition, amount):
        @pl.when(condition)
        def _():
            pl.semaphore_wait(barrier, amount)

    for o in (1, 2):
        greet(places[o], late & jnp.logical_not(near_front[o]))
    for o in (3, 4):
        greet(places[o], late | (early & jnp.logical_not(near_lead[o])))
    greet(twin, paired)

    load_cut = pltpu.make_async_copy(cut_hbm, cut, small_sem.at[0])
    load_cut.start()
    load_atom = pltpu.make_async_copy(atom_hbm, atom, small_sem.at[1])
    load_atom.start()
    sources = {H: ham.at[0, 0], S: inv.at[0, 0], R: den.at[0, 0, 0], I: den.at[1, 0, 0]}
    loads = {}
    for m in (H, S, I, R):
        loads[m] = pltpu.make_async_copy(sources[m], own.at[m], in_sem.at[m])
        loads[m].start()
    load_slope = pltpu.make_async_copy(der.at[:, 0, 0], slope, der_sem)
    load_slope.start()

    load_cut.wait()
    keep = [None] + [cut[0, 0, o].astype(f32) for o in (1, 2, 3, 4)]

    def prepare(m):
        loads[m].wait()
        for o in range(5):
            block = own[m, o]
            if o > 0:
                block = block * keep[o]
                send[m, o - 1, 1] = block
                own[m, o] = block
            else:
                for p in range(4):
                    send[m, p, 0] = block
            high, low = split(block)
            columns = pl.ds(o * B, B)
            if m == H:
                hb_h[:, columns] = high
                hb_l[:, columns] = low
            else:
                rows = pl.ds((m - 1) * B, B)
                left_h[o, rows, :] = high
                left_l[o, rows, :] = low
                if m == S:
                    for t in range(2):
                        pair_h[t, pl.ds(B, B), columns] = high
                        pair_l[t, pl.ds(B, B), columns] = low
                else:
                    pair_h[m - 2, pl.ds(0, B), columns] = high
                    pair_l[m - 2, pl.ds(0, B), columns] = low

    def copy(m, o):
        return pltpu.make_async_remote_copy(
            src_ref=send.at[m, o - 1],
            dst_ref=recv.at[m, opposite[o] - 1],
            send_sem=send_sem.at[m, o - 1],
            recv_sem=recv_sem.at[m, opposite[o] - 1],
            device_id=places[o],
            device_id_type=MESH,
        )

    def arrived(m, o):
        copy(m, opposite[o]).wait_recv()

    order = (3, 4, 1, 2)

    await_greetings(early, 2 - number(beside) + number(paired))
    await_greetings(lead, 2)
    for o in (3, 4):
        greet(places[o], lead)
    greet(places[1], front)
    greet(cousin, paired)
    prepare(H)
    await_greetings(late, 4 + number(carrier) + 2 * number(served))
    for o in (1, 2):
        greet(places[o], late & near_front[o])
    greet(giver, carrier)
    greet(taker, carrier)
    greet(ahead, served)
    greet(helper, served)

    def hand_on(m):
        return pltpu.make_async_remote_copy(
            src_ref=send.at[m, 1],
            dst_ref=passing.at[m],
            send_sem=send_sem.at[m, 1],
            recv_sem=pass_sem.at[m],
            device_id=twin if m in BY_TWIN else cousin,
            device_id_type=MESH,
        )

    def forward(m):
        return pltpu.make_async_remote_copy(
            src_ref=passing.at[m],
            dst_ref=recv.at[m, 0],
            send_sem=forward_sem.at[m],
            recv_sem=recv_sem.at[m, 0],
            device_id=behind if m in BY_TWIN else taker,
            device_id_type=MESH,
        )

    def transfer(m, o, condition):
        @pl.when(condition)
        def _():
            copy(m, o).start()

    def pass_on(m):
        hand_on(m).wait_recv()
        forward(m).start()

    def launch(m):
        if m == H:
            for o in (1, 2):
                transfer(m, o, late)
        for o in (3, 4):
            transfer(m, o, jnp.logical_not(early & near_lead[o]) if m == H else front & jnp.logical_not(early & near_lead[o]))
        if m in BY_TWIN:

            @pl.when(paired)
            def _():
                hand_on(m).start()

    launch(H)
    for m in (S, I):
        prepare(m)
        launch(m)
    prepare(R)
    for o in (3, 4):
        transfer(R, o, front & jnp.logical_not(early & near_lead[o]))

    await_greetings(front, 1 + number(paired))
    for m in (H, S, I, R):
        transfer(m, 1, front)
        if m not in BY_TWIN:

            @pl.when(paired)
            def _():
                hand_on(m).start()

    for o in (3, 4):
        greet(places[o], early & near_lead[o])
    await_greetings(beside, 1)
    for o in (3, 4):
        for m in (H, S, I, R):
            transfer(m, o, early & near_lead[o])

    greet(places[2], front)
    greet(behind, paired)
    await_greetings(front, 1 + number(paired))
    for m in (H, S, I):
        transfer(m, 2, front & jnp.logical_not(paired))
    for m in BY_TWIN:

        @pl.when(paired)
        def _():
            pass_on(m)

    for o in range(5):
        columns = pl.ds(o * B, B)
        hams[o] = multiply(left_h[0], left_l[0], hb_h[:, columns], hb_l[:, columns])

    @pl.when(late)
    def _():
        for o in (1, 2, 3, 4):
            copy(H, o).wait_send()
            copy(S, o).start()
            copy(I, o).start()

    transfer(R, 1, last)

    for o in order:
        arrived(H, o)
        near = jnp.concatenate([recv[H, o - 1, 0], recv[H, o - 1, 1]], axis=1)
        bh, bl = split(near)
        part = multiply(left_h[o], left_l[o], bh, bl)
        hams[0] += part[:, B:]
        block = (hams[o] + part[:, :B]) * keep[o]
        for t, sign in ((0, 1.0), (1, -1.0), (2, -1.0)):
            high, low = split(block[t * B : (t + 1) * B] * sign)
            mixed_h[o, :, pl.ds(t * B, B)] = high
            mixed_l[o, :, pl.ds(t * B, B)] = low
    for t, sign in ((0, 1.0), (1, -1.0), (2, -1.0)):
        high, low = split(hams[0, pl.ds(t * B, B), :] * sign)
        mixed_h[0, :, pl.ds(t * B, B)] = high
        mixed_l[0, :, pl.ds(t * B, B)] = low

    def lefts(o, m):
        t = m - 1
        return (
            jnp.concatenate([mixed_h[o, :, pl.ds(0, B)], mixed_h[o, :, pl.ds(t * B, B)]], axis=1),
            jnp.concatenate([mixed_l[o, :, pl.ds(0, B)], mixed_l[o, :, pl.ds(t * B, B)]], axis=1),
        )

    def columns_to(o):
        return pltpu.make_async_remote_copy(
            src_ref=col_send.at[o - 1],
            dst_ref=col_recv.at[o - 1],
            send_sem=cs_sem.at[o - 1],
            recv_sem=cr_sem.at[o - 1],
            device_id=places[o],
            device_id_type=MESH,
        )

    def new_real(o):
        block = own[R, o] + time_step * comm[o]
        out[0, 0, 0, o] = block
        for c in range(3):
            col_send[o - 1, pl.ds(c, 1), :] = jnp.sum(block * slope[c, o], axis=0, keepdims=True)
        columns_to(o).start()
        transfer(R, o, late & jnp.logical_not(last) if o == 1 else late)

    def near(m, o):
        return split(jnp.concatenate([recv[m, o - 1, 0], recv[m, o - 1, 1]], axis=1))

    def mixed(o, t):
        return mixed_h[o, :, pl.ds(t * B, B)], mixed_l[o, :, pl.ds(t * B, B)]

    def commutator(m):
        ah, al = lefts(0, m)
        for o in range(5):
            columns = pl.ds(o * B, B)
            comm[o] = multiply(ah, al, pair_h[m - 2, :, columns], pair_l[m - 2, :, columns])
        for o in (1, 3, 4, 2):
            if m == I:
                arrived(S, o)
                sh, sl = near(S, o)
                side_h[o - 1], side_l[o - 1] = sh, sl
                arrived(I, o)
                bh, bl = near(I, o)
                part = multiply(*lefts(o, m), jnp.concatenate([bh, sh], axis=0), jnp.concatenate([bl, sl], axis=0))
                comm[0] += part[:, B:]
                comm[o] = (comm[o] + part[:, :B]) * keep[o]
                new_real(o)
            else:
                part = multiply(*mixed(o, 1), side_h[o - 1], side_l[o - 1])
                comm[0] += part[:, B:]
                comm[o] += part[:, :B]
        if m == R:
            for o in (1, 3, 4, 2):
                arrived(R, o)
                part = multiply(*mixed(o, 0), *near(R, o))
                comm[0] += part[:, B:]
                out[1, 0, 0, o] = own[I, o] - time_step * ((comm[o] + part[:, :B]) * keep[o])

    load_slope.wait()
    @pl.when(carrier)
    def _():
        pl.semaphore_wait(barrier, 1)
        for m in (I, R, S, H):
            if m not in BY_TWIN:
                pass_on(m)

    commutator(I)
    transfer(R, 2, front & jnp.logical_not(paired))
    out[0, 0, 0, 0] = own[R, 0] + time_step * comm[0]

    rows, cols = [], []
    for c in range(3):
        weighted = out[0, 0, 0, 0] * slope[c, 0]
        cols.append(jnp.sum(weighted, axis=0, keepdims=True))
        for o in order:
            weighted = weighted + out[0, 0, 0, o] * slope[c, o]
        rows.append(jnp.sum(weighted.T, axis=0, keepdims=True))
    orbital = jnp.concatenate(rows, axis=0) + jnp.concatenate(cols, axis=0)
    load_atom.wait()
    members = (
        jnp.broadcast_to(atom[0], (ATOMS, B)) == lax.broadcasted_iota(jnp.int32, (ATOMS, B), 0)
    ).astype(f32)
    commutator(R)
    out[1, 0, 0, 0] = own[I, 0] - time_step * comm[0]

    for o in order:
        columns_to(o).wait_recv()
    for o in order:
        orbital = orbital + col_recv[o - 1, pl.ds(0, 3), :]
    total = lax.dot_general(
        orbital, members, (((1,), (1,)), ((), ())),
        precision=lax.Precision.HIGHEST, preferred_element_type=f32,
    )
    for c in range(3):
        forces[0, c] = total[c : c + 1]
    for m in (S, I, R):
        for o in order:
            copy(m, o).wait_send()

    @pl.when(front)
    def _():
        for o in order:
            copy(H, o).wait_send()

    for o in order:
        columns_to(o).wait_send()

    for m in (H, S, I, R):

        @pl.when(paired if m in BY_TWIN else carrier)
        def _():
            forward(m).wait_send()


def local(hamiltonian, inverse_margin, density, cutoff, derivative, atom_of):
    hbm = pl.BlockSpec(memory_space=pltpu.HBM)
    vmem = pl.BlockSpec(memory_space=pltpu.VMEM)
    dma = pltpu.SemaphoreType.DMA
    density, forces = pl.pallas_call(
        kernel,
        out_shape=(
            jax.ShapeDtypeStruct((2, 1, 1, 5, B, B), f32),
            jax.ShapeDtypeStruct((1, 3, 1, ATOMS), f32),
        ),
        in_specs=[hbm] * 6,
        out_specs=(vmem, vmem),
        scratch_shapes=[
            pltpu.SMEM((1, 1, 5), jnp.int32),
            pltpu.VMEM((1, 1, B), jnp.int32),
            pltpu.VMEM((4, 5, B, B), f32),
            pltpu.VMEM((3, 5, B, B), f32),
            pltpu.VMEM((4, 4, 2, B, B), f32),
            pltpu.VMEM((4, 4, 2, B, B), f32),
            pltpu.VMEM((4, 8, B), f32),
            pltpu.VMEM((4, 8, B), f32),
            pltpu.VMEM((5, 3 * B, B), bf16),
            pltpu.VMEM((5, 3 * B, B), bf16),
            pltpu.VMEM((B, 5 * B), bf16),
            pltpu.VMEM((B, 5 * B), bf16),
            pltpu.VMEM((2, 2 * B, 5 * B), bf16),
            pltpu.VMEM((2, 2 * B, 5 * B), bf16),
            pltpu.VMEM((5, 3 * B, B), f32),
            pltpu.VMEM((5, B, 3 * B), bf16),
            pltpu.VMEM((5, B, 3 * B), bf16),
            pltpu.VMEM((5, B, B), f32),
            dma((4,)),
            dma((2,)),
            dma,
            dma((4, 4)),
            dma((4, 4)),
            dma((4,)),
            dma((4,)),
            pltpu.VMEM((4, 2, B, B), f32),
            dma((4,)),
            dma((4,)),
            pltpu.VMEM((4, B, 2 * B), bf16),
            pltpu.VMEM((4, B, 2 * B), bf16),
        ],
        compiler_params=pltpu.CompilerParams(
            collective_id=0, has_side_effects=True, vmem_limit_bytes=40 * 1024 * 1024
        ),
        name="cell",
    )(*[
        pltpu.with_memory_space_constraint(x, pltpu.HBM)
        for x in (hamiltonian, inverse_margin, density, cutoff, derivative, atom_of)
    ])
    return density, -forces.reshape(1, 1, 3, ATOMS)


def solution(mesh):
    placed = (
        P("gx", "gy", None, None, None),
        P("gx", "gy", None, None, None),
        P(None, "gx", "gy", None, None, None),
        P("gx", "gy", None),
        P(None, "gx", "gy", None, None, None),
        P("gx", "gy", None),
    )
    return jax.shard_map(
        local,
        mesh=mesh,
        in_specs=placed,
        out_specs=(P(None, "gx", "gy", None, None, None), P("gx", "gy", None, None)),
        check_vma=False,
    )
```
